512 devices in a mesh: stream: 16 (over x, y), cross: 32 (over z, core).
Axes of the slice: x: 4, y: 4, z: 16, core: 2. Of those that a mesh axis runs over, the one named last changes fastest.
Arguments:
- inflow: float32 [2, 8, 5, 256, 256], P(None, None, None, 'cross'), may hold values from -6 to 6
- source_shape: float32 [5, 256, 256], P(None, 'cross'), may hold values from -6 to 6
- source_amp: float32 [16, 2, 8], P('stream'), may hold values from -3 to 3
- coupling: float32 [4, 4, 5, 5], replicated, may hold values from -0.4375 to 0.4375
- omega: float32 [8], replicated, may hold values from 0.05 to 0.25
- rec_coef: float32 [4], replicated, may hold values from 0.7 to 1
- rec_order: int32 [4], replicated, may hold values from 0 to 3, each once
- station_zone: int32 [16], P('stream'), may hold values from 0 to 3
- solid_mask: int32 [256, 256], P('cross'), may hold values from 0 to 1, as said below
Outputs:
- group_exits: float32 [16, 2, 8, 5, 256, 256], P('stream', None, None, None, 'cross')
The draws below stay inside these ranges and needn't reach their ends.
Inputs may be any that keep to these rules, and one draw needn't show every extreme that they name: rec_order holds each of 0 .. 3 once. `solid_mask`: 1 marks a solid cell, 0 a fluid cell.
All inputs are finite; a program needn't handle non-finite values.
Results may differ from the reference program's by a relative error of at most 0.00011.
Values sent between devices are 32-bit elements; how exact they have to be, the bound alone decides.
A program may use at most 64 MiB of HBM per device.

```python
import math
import jax
import jax.numpy as jnp
from jax import lax

NVAR = 5
FREQ = 8
NZ = 256
STN_DEV = 1
RECUR = 4
ZONES = 4
NY = 256
STATIONS = 16
N_STREAM = 16


def draw_solid_mask(key, part):
    subkeys = jax.random.split(jax.random.fold_in(key, 7), 5)
    shorter = min(NY, NZ)
    row_ids = jnp.arange(NY, dtype=jnp.int32)[:, None]
    col_ids = jnp.arange(NZ, dtype=jnp.int32)[None, :]
    centre_row = NY // 2 + jax.random.randint(subkeys[0], (), -(NY // 8), NY // 8 + 1)
    centre_col = NZ // 2 + jax.random.randint(subkeys[1], (), -(NZ // 8), NZ // 8 + 1)
    row_gap = row_ids - centre_row
    col_gap = col_ids - centre_col
    distance = row_gap * row_gap + col_gap * col_gap
    inner_radius = jax.random.randint(subkeys[2], (), shorter // 8, shorter // 4 + 1)
    thickness = jax.random.randint(subkeys[3], (), max(1, shorter // 32), max(2, shorter // 16) + 1)
    outer_radius = inner_radius + thickness
    nozzle_lip = (distance >= inner_radius * inner_radius) & (distance < outer_radius * outer_radius)
    debris = jax.random.randint(subkeys[4], (NY, NZ), 0, 12) == 0
    return (nozzle_lip | debris).astype(jnp.int32)


def touch_ends(result, key, low, largest):
    longest = result.shape.index(max(result.shape))
    spots = []
    for shift in (0, 1):
        where = [jax.random.randint(jax.random.fold_in(key, axis), (), 0, length) for axis, length in enumerate(result.shape)]
        where[longest] = (where[longest] + shift) % result.shape[longest]
        spots.append(tuple(where))
    return result.at[spots[0]].set(low).at[spots[1]].set(largest)


def steps_of(own_key, dims, cuts, least, high):
    def one(position, parts):
        heights = jax.random.uniform(jax.random.fold_in(jax.random.fold_in(own_key, 6), position), (parts,), jnp.float32, least / len(cuts), high / len(cuts))
        return jnp.repeat(jnp.exp(heights), dims[position] // parts).reshape((-1,) + (1,) * (len(dims) - position - 1))

    gain = one(*cuts[0])
    for cut in cuts[1:]:
        gain = gain * one(*cut)
    return gain


def scatter_about(stream_key, shape, spread, bound, shards=(), kind=jnp.bfloat16):
    drawn = spread * jax.random.normal(stream_key, shape, jnp.float32)
    if shards:
        drawn = drawn * steps_of(stream_key, shape, shards, -0.22, 0.18)
    return jnp.clip(drawn, -bound, bound).astype(kind)


def setup_inputs(seed: int = 0) -> dict:
    key_list = jax.random.split(jax.random.key(seed), 10)
    inflow = scatter_about(key_list[0], (2, FREQ, NVAR, NY, NZ), 1.0, 6.0, ((3, 32),), jnp.float32)
    source_shape = scatter_about(key_list[1], (NVAR, NY, NZ), 1.0, 6.0, ((1, 32),), jnp.float32)
    source_amp = scatter_about(key_list[2], (STATIONS, 2, FREQ), 0.2, 3.0, ((0, 16),), jnp.float32)
    coupling = scatter_about(key_list[3], (ZONES, 4, NVAR, NVAR), (40 * NVAR) ** -0.5, 0.4375, (), jnp.float32)
    omega = jnp.clip(jnp.exp(jax.random.uniform(key_list[4], (FREQ,), jnp.float32, math.log(0.05), math.log(0.25))), 0.05, 0.25)
    rec_coef = jnp.clip(jnp.exp(jax.random.uniform(key_list[5], (RECUR,), jnp.float32, math.log(0.7), math.log(1.0))), 0.7, 1.0)
    rec_order = jax.random.permutation(key_list[6], RECUR).astype(jnp.int32)
    station_zone = touch_ends(jax.random.randint(key_list[7], (STATIONS,), 0, ZONES), jax.random.fold_in(key_list[7], 1), 0, ZONES - 1).astype(jnp.int32)
    solid_mask = draw_solid_mask(jax.random.fold_in(key_list[9], 71), 0)
    return dict(inflow=inflow, source_shape=source_shape, source_amp=source_amp, coupling=coupling, omega=omega, rec_coef=rec_coef, rec_order=rec_order, station_zone=station_zone, solid_mask=solid_mask)


viscosity = 0.05
penalty = 0.5
damping = 0.03


def station_operators(matrices):
    var_count = matrices.shape[-1]
    advect_rows = 0.5 * (matrices[0] + matrices[0].T)
    advect_cols = 0.5 * (matrices[1] + matrices[1].T)
    rotation_part = 0.5 * (matrices[2] - matrices[2].T)
    viscous = viscosity * (jnp.eye(var_count, dtype=jnp.float32) + jnp.dot(matrices[3], matrices[3].T, precision=lax.Precision.HIGHEST))
    return jnp.stack([advect_rows, advect_cols, rotation_part, viscous])


def apply_operator(padded, operators, damp_field, frequency):
    center = padded[:, :, :, 1:-1, :]
    row_next = padded[:, :, :, 2:, :]
    row_prev = padded[:, :, :, :-2, :]
    col_next = jnp.roll(center, -1, axis=4)
    col_prev = jnp.roll(center, 1, axis=4)
    stencil = jnp.stack([0.5 * (row_next - row_prev), 0.5 * (col_next - col_prev), center,
                         row_next + row_prev + col_next + col_prev - 4.0 * center])
    coupled = jnp.einsum("kvw,krfwyz->rfvyz", operators, stencil, precision=lax.Precision.HIGHEST)
    spinning = frequency[:, None, None, None]
    turning = jnp.stack([spinning * center[1], -spinning * center[0]])
    return coupled - damp_field * center + turning


def level_factors(rec_coef, rec_order):
    levels = rec_coef.shape[0]
    picked = jnp.sum(jnp.where(rec_order[:, None] == jnp.arange(levels, dtype=jnp.int32)[None, :],
                               rec_coef[None, :], jnp.zeros((), jnp.float32)), axis=1)
    return picked / (levels - jnp.arange(levels, dtype=jnp.int32)).astype(jnp.float32)


def reference(inflow, source_shape, source_amp, coupling, omega, rec_coef, rec_order, station_zone, solid_mask):
    damp_field = penalty * solid_mask.astype(jnp.float32) + damping
    factors = level_factors(rec_coef, rec_order)
    marched = inflow
    group_exits = []
    for group_index in range(N_STREAM):
        for station_pos in range(STN_DEV):
            station = group_index * STN_DEV + station_pos
            operators = station_operators(coupling[station_zone[station]])
            current = marched
            for depth_step in range(RECUR):
                padded = jnp.pad(current, ((0, 0), (0, 0), (0, 0), (1, 1), (0, 0)))
                current = marched + factors[depth_step] * apply_operator(padded, operators, damp_field, omega)
            marched = current + source_amp[station][:, :, None, None, None] * source_shape[None, None]
        group_exits.append(marched)
    return jnp.stack(group_exits)
```

```python
import functools

import jax
import jax.numpy as jnp
from jax import lax
from jax.experimental import pallas as pl
from jax.experimental.pallas import tpu as pltpu
from jax.sharding import PartitionSpec as P

viscosity = 0.05
penalty = 0.5
damping = 0.03

MESH = pl.DeviceIdType.MESH
ROWS = 8
OWN = 4
PAIRS = 12
STEP = 2


def kernel(
    dims,
    inflow,
    shape,
    amp,
    coupling,
    omega,
    rec_coef,
    rec_order,
    zone,
    mask,
    out,
    nat_in,
    shape_in,
    mask_in,
    tile,
    amp_all,
    zone_all,
    coef,
    diag,
    field,
    frame_src,
    frame_damp,
    sent,
    got,
    sent_fix,
    got_fix,
    exits,
    in_sem,
    gather_send,
    gather_recv,
    halo_send,
    halo_recv,
    fix_send,
    fix_recv,
    exit_send,
    exit_recv,
    local_sem,
):
    streams, crosses, freqs, nvar, zones, stations = dims
    me = lax.axis_index("stream")
    row = lax.axis_index("cross")
    freq = lax.rem(me, freqs)
    part = lax.div(me, freqs)
    above = row > 0
    below = row < crosses - 1

    sub = lax.broadcasted_iota(jnp.int32, (8, 128), 0)
    lane = lax.broadcasted_iota(jnp.int32, (8, 128), 1)
    top = (sub & 2) == 0
    real = (sub & 1) == 0
    first = lane == 0
    last = lane == 127

    def swap_rows(x):
        return jnp.where(top, pltpu.roll(x, 6, 0), pltpu.roll(x, 2, 0))

    def swap_parts(x):
        return jnp.where(real, pltpu.roll(x, 7, 0), pltpu.roll(x, 1, 0))

    loads = [
        pltpu.make_async_copy(inflow.at[:, freq], nat_in, in_sem.at[0]),
        pltpu.make_async_copy(shape, shape_in, in_sem.at[1]),
        pltpu.make_async_copy(mask, mask_in, in_sem.at[2]),
        pltpu.make_async_copy(amp.at[0], amp_all.at[me], in_sem.at[3]),
        pltpu.make_async_copy(zone, zone_all.at[me], in_sem.at[4]),
    ]
    for load in loads:
        load.start()

    barrier = pltpu.get_barrier_semaphore()

    def greet(k, carry):
        pl.semaphore_signal(
            barrier,
            inc=1,
            device_id=(lax.rem(me + k, streams), row),
            device_id_type=MESH,
        )
        return carry

    @pl.when(above)
    def _():
        pl.semaphore_signal(barrier, inc=1, device_id=(me, row - 1), device_id_type=MESH)

    @pl.when(below)
    def _():
        pl.semaphore_signal(barrier, inc=1, device_id=(me, row + 1), device_id_type=MESH)

    lax.fori_loop(1, streams, greet, 0)

    @pl.when(row == 0)
    def _():
        got[0, 0] = jnp.zeros_like(got[0, 0])
        got[1, 0] = jnp.zeros_like(got[1, 0])
        got_fix[0] = jnp.zeros_like(got_fix[0])

    @pl.when(row == crosses - 1)
    def _():
        got[0, 1] = jnp.zeros_like(got[0, 1])
        got[1, 1] = jnp.zeros_like(got[1, 1])
        got_fix[1] = jnp.zeros_like(got_fix[1])

    per_zone = 4 * nvar * nvar
    side = jnp.where(top, 1.0, -1.0).astype(jnp.float32)

    def zone_coef(z, carry):
        def put(kind, i, w, value):
            coef[z * per_zone + (kind * nvar + i) * nvar + w] = value

        def full(value):
            return jnp.full((8, 128), value, jnp.float32)

        for i in range(nvar):
            for w in range(i, nvar):
                rows_iw = full(0.25 * (coupling[z, 0, i, w] + coupling[z, 0, w, i])) * side
                cols_iw = full(0.25 * (coupling[z, 1, i, w] + coupling[z, 1, w, i]))
                dot = coupling[z, 3, i, 0] * coupling[z, 3, w, 0]
                for k in range(1, nvar):
                    dot = dot + coupling[z, 3, i, k] * coupling[z, 3, w, k]
                if i == w:
                    dot = dot + 1.0
                visc = viscosity * dot
                turn = 0.5 * (coupling[z, 2, i, w] - coupling[z, 2, w, i])
                put(0, i, w, rows_iw)
                put(1, i, w, cols_iw)
                put(3, i, w, full(visc))
                put(2, i, w, full(turn - 4.0 * visc))
                if i != w:
                    put(0, w, i, rows_iw)
                    put(1, w, i, cols_iw)
                    put(3, w, i, full(visc))
                    put(2, w, i, full(-turn - 4.0 * visc))
        return carry

    lax.fori_loop(0, zones, zone_coef, 0)

    f0, f1, f2, f3 = [rec_coef[rec_order[k]] * (1.0 / (4 - k)) for k in range(4)]
    spin = omega[freq]
    c1 = f3
    c2 = c1 * f2
    c3 = c2 * f1
    c4 = c3 * f0
    spin2 = spin * spin
    spin3 = spin2 * spin
    re_part = [1.0 - c2 * spin2 + c4 * spin2 * spin2, c1 - 3.0 * c3 * spin2, c2 - 6.0 * c4 * spin2, c3, c4]
    im_part = [c3 * spin3 - c1 * spin, 4.0 * c4 * spin3 - 2.0 * c2 * spin, -3.0 * c3 * spin, -4.0 * c4 * spin]
    flip = jnp.where(real, 1.0, -1.0).astype(jnp.float32)
    for k in range(5):
        coef[zones * per_zone + k] = jnp.full((8, 128), re_part[k], jnp.float32)
    for k in range(4):
        coef[zones * per_zone + 5 + k] = jnp.full((8, 128), im_part[k], jnp.float32) * flip

    def pairs_of(slot, get):
        for p in range(2):
            for h in range(2):
                tile[slot, pl.ds(4 * h + p, 8, stride=8), :] = get(p, h)
        return [
            jnp.where(top, tile[slot, 8 * k : 8 * k + 8], swap_rows(tile[slot, 56 - 8 * k : 64 - 8 * k]))
            for k in range(OWN)
        ]

    for load in loads:
        load.wait()
    for v in range(nvar):
        own = pairs_of(v, lambda p, h: nat_in[p, v, :, 128 * h : 128 * h + 128])
        for k in range(OWN):
            field[0, v, 8 + k] = own[k]
            sent[0, v * OWN + k] = own[k]
    for v in range(nvar):
        own = pairs_of(v, lambda p, h: shape_in[v, :, 128 * h : 128 * h + 128])
        for k in range(OWN):
            frame_src[v, 8 + k] = own[k]
            sent_fix[v * OWN + k] = own[k]
    own = pairs_of(
        0,
        lambda p, h: penalty * mask_in[:, 128 * h : 128 * h + 128].astype(jnp.float32) + damping,
    )
    for k in range(OWN):
        frame_damp[8 + k] = own[k]
        sent_fix[nvar * OWN + k] = own[k]

    pl.semaphore_wait(barrier, streams - 1 + above.astype(jnp.int32) + below.astype(jnp.int32))

    def gather_copies(k):
        peer = lax.rem(me + k, streams)
        return (
            pltpu.make_async_remote_copy(
                zone, zone_all.at[me], gather_send.at[0, k], gather_recv.at[0, k],
                device_id=(peer, row), device_id_type=MESH,
            ),
            pltpu.make_async_remote_copy(
                amp.at[0], amp_all.at[me], gather_send.at[1, k], gather_recv.at[1, k],
                device_id=(peer, row), device_id_type=MESH,
            ),
        )

    def gather_start(k, carry):
        for copy in gather_copies(k):
            copy.start()
        return carry

    lax.fori_loop(1, streams, gather_start, 0)

    def halo_copies(exchange, slot):
        up = pltpu.make_async_remote_copy(
            sent.at[slot], got.at[slot, 1], halo_send.at[slot, 0], halo_recv.at[slot, 1],
            device_id=(me, row - 1), device_id_type=MESH,
        )
        down = pltpu.make_async_remote_copy(
            sent.at[slot], got.at[slot, 0], halo_send.at[slot, 1], halo_recv.at[slot, 0],
            device_id=(me, row + 1), device_id_type=MESH,
        )
        return up, down

    fix_up = pltpu.make_async_remote_copy(
        sent_fix, got_fix.at[1], fix_send.at[0], fix_recv.at[1],
        device_id=(me, row - 1), device_id_type=MESH,
    )
    fix_down = pltpu.make_async_remote_copy(
        sent_fix, got_fix.at[0], fix_send.at[1], fix_recv.at[0],
        device_id=(me, row + 1), device_id_type=MESH,
    )

    def halo_start(exchange, slot):
        up, down = halo_copies(exchange, slot)

        @pl.when(above)
        def _():
            up.start()

        @pl.when(below)
        def _():
            down.start()

    def halo_wait_send(slot):
        up, down = halo_copies(0, slot)

        @pl.when(above)
        def _():
            up.wait_send()

        @pl.when(below)
        def _():
            down.wait_send()

    def halo_wait_recv(slot):
        up, down = halo_copies(0, slot)

        @pl.when(above)
        def _():
            down.wait_recv()

        @pl.when(below)
        def _():
            up.wait_recv()

    @pl.when(above)
    def _():
        fix_up.start()

    @pl.when(below)
    def _():
        fix_down.start()

    halo_start(0, 0)

    def halo_pairs(before, after):
        outer = [jnp.where(top, before(k), after(k)) for k in range(OWN)]
        inner = [swap_rows(jnp.where(top, after(k), before(k))) for k in range(OWN)]
        return outer + inner[::-1]

    @pl.when(above)
    def _():
        fix_up.wait_send()
        fix_down.wait_recv()

    @pl.when(below)
    def _():
        fix_down.wait_send()
        fix_up.wait_recv()

    for v in range(nvar):
        halo = halo_pairs(lambda k: got_fix[0, v * OWN + k], lambda k: got_fix[1, v * OWN + k])
        for j in range(8):
            frame_src[v, j] = halo[j]
    halo = halo_pairs(
        lambda k: got_fix[0, nvar * OWN + k], lambda k: got_fix[1, nvar * OWN + k]
    )
    for j in range(8):
        frame_damp[j] = halo[j]

    def zone_diag(z, carry):
        for i in range(nvar):
            center = coef[z * per_zone + (2 * nvar + i) * nvar + i]
            for j in range(1, PAIRS):
                diag[(z * nvar + i) * PAIRS + j] = center - frame_damp[j]
        return carry

    lax.fori_loop(0, zones, zone_diag, 0)

    inside = jnp.where(top, above.astype(jnp.float32), below.astype(jnp.float32))

    def gather_wait(k, carry):
        for copy in gather_copies(k):
            copy.wait()
        return carry

    lax.fori_loop(1, streams, gather_wait, 0)

    def exit_copy(n):
        return pltpu.make_async_remote_copy(
            exits.at[n], out.at[0, part, freq], exit_send.at[n], exit_recv.at[me],
            device_id=(n, row), device_id_type=MESH,
        )

    def exit_local(n):
        return pltpu.make_async_copy(exits.at[n], out.at[0, part, freq], local_sem)

    def march(n, start):
        here = jnp.max(zone_all[n])
        base = here * per_zone
        dbase = here * (nvar * PAIRS)
        amps = amp_all[n]
        mine = lax.broadcasted_iota(jnp.int32, amps.shape, 1) == freq
        amps = jnp.sum(jnp.where(mine, amps, 0.0), axis=1, keepdims=True)
        weight = jnp.where(real, amps[0:1], amps[1:2])
        for level in range(4):
            lo = start + 1 + level
            js = list(range(lo, PAIRS))
            chunks = [js[a : a + 2] for a in range(len(js) % 2 and 1 or 0, len(js), 2)]
            if len(js) % 2:
                chunks = [js[:1]] + chunks
            for chunk in chunks:
                feats = {}
                for v in range(nvar):
                    vs = {
                        j: field[level, v, j] for j in range(chunk[0] - 1, chunk[-1] + 2)
                    }
                    for j in chunk:
                        x = vs[j]
                        other = pltpu.roll(x, 4, 0)
                        east = pltpu.roll(jnp.where(first, other, x), 127, 1)
                        west = pltpu.roll(jnp.where(last, other, x), 1, 1)
                        feats[v, j] = (
                            vs[j + 1] - vs[j - 1],
                            east - west,
                            x,
                            (vs[j + 1] + vs[j - 1]) + (east + west),
                        )
                for i in range(nvar):
                    total = {
                        j: diag[dbase + i * PAIRS + j] * feats[i, j][2] for j in chunk
                    }
                    for kind in range(4):
                        for w in range(nvar):
                            if kind == 2 and w == i:
                                continue
                            g = coef[base + (kind * nvar + i) * nvar + w]
                            for j in chunk:
                                total[j] = total[j] + g * feats[w, j][kind]
                    for j in chunk:
                        value = total[j]
                        if j == 7:
                            value = value * inside
                        if level < 3:
                            field[level + 1, i, j] = value
                            if j == PAIRS - 1:
                                field[level + 1, i, PAIRS] = swap_rows(value)
                        else:
                            u = [field[k, i, j] for k in range(4)]
                            b = zones * per_zone
                            a_sum = coef[b] * u[0] + coef[b + 4] * value
                            b_sum = coef[b + 5] * u[0]
                            for k in range(1, 4):
                                a_sum = a_sum + coef[b + k] * u[k]
                                b_sum = b_sum + coef[b + 5 + k] * u[k]
                            new = a_sum + swap_parts(b_sum) + weight * frame_src[i, j]
                            field[0, i, j] = new
                            if j == PAIRS - 1:
                                field[0, i, PAIRS] = swap_rows(new)

    def leave(n):
        for v in range(nvar):
            for k in range(OWN):
                x = field[0, v, 8 + k]
                tile[v, 8 * k : 8 * k + 8] = x
                tile[v, 56 - 8 * k : 64 - 8 * k] = swap_rows(x)
            for h in range(2):
                even = tile[v, pl.ds(4 * h, 8, stride=8), :]
                odd = tile[v, pl.ds(4 * h + 1, 8, stride=8), :]
                exits[n, v, :, 128 * h : 128 * h + 128] = jnp.where(part == 0, even, odd)

        @pl.when(n == me)
        def _():
            exit_local(n).start()

        @pl.when(n != me)
        def _():
            exit_copy(n).start()

    for v in range(nvar):
        field[0, v, PAIRS] = swap_rows(field[0, v, PAIRS - 1])

    stages = stations // STEP

    def stage(t, carry):
        slot = lax.rem(t, 2)
        other = 1 - slot
        halo_wait_recv(slot)
        for v in range(nvar):
            halo = halo_pairs(lambda k: got[slot, 0, v * OWN + k], lambda k: got[slot, 1, v * OWN + k])
            for j in range(8):
                field[0, v, j] = halo[j]
        march(2 * t, 0)
        leave(2 * t)
        march(2 * t + 1, 4)

        @pl.when(t < stages - 1)
        def _():
            @pl.when(t > 0)
            def _():
                halo_wait_send(other)

            for v in range(nvar):
                for k in range(OWN):
                    sent[other, v * OWN + k] = field[0, v, 8 + k]
            halo_start(t + 1, other)

        leave(2 * t + 1)
        return carry

    lax.fori_loop(0, stages, stage, 0)

    if stages > 1:
        halo_wait_send((stages - 2) % 2)
    halo_wait_send((stages - 1) % 2)

    def finish(n, carry):
        @pl.when(n == me)
        def _():
            exit_local(n).wait()

        @pl.when(n != me)
        def _():
            exit_copy(n).wait_send()
            pltpu.make_async_remote_copy(
                exits.at[n], out.at[0, part, freq], exit_send.at[n], exit_recv.at[n],
                device_id=(n, row), device_id_type=MESH,
            ).wait_recv()

        return carry

    lax.fori_loop(0, streams, finish, 0)


def on_device(dims, inflow, shape, amp, coupling, omega, rec_coef, rec_order, zone, mask):
    streams, crosses, freqs, nvar, zones, stations = dims
    cols = inflow.shape[-1]
    anywhere = pl.BlockSpec(memory_space=pl.ANY)
    scalars = pl.BlockSpec(memory_space=pltpu.SMEM)
    f32 = jnp.float32
    dma = pltpu.SemaphoreType.DMA
    return pl.pallas_call(
        functools.partial(kernel, dims),
        out_shape=jax.ShapeDtypeStruct((1, 2, freqs, nvar, ROWS, cols), f32),
        in_specs=[anywhere, anywhere, anywhere, scalars, scalars, scalars, scalars, anywhere, anywhere],
        out_specs=anywhere,
        scratch_shapes=[
            pltpu.VMEM((2, nvar, ROWS, cols), f32),
            pltpu.VMEM((nvar, ROWS, cols), f32),
            pltpu.VMEM((ROWS, cols), jnp.int32),
            pltpu.VMEM((nvar, 64, 128), f32),
            pltpu.VMEM((streams, 2, freqs), f32),
            pltpu.VMEM((streams, 1, 1), jnp.int32),
            pltpu.VMEM((zones * 4 * nvar * nvar + 9, 8, 128), f32),
            pltpu.VMEM((zones * nvar * PAIRS, 8, 128), f32),
            pltpu.VMEM((4, nvar, PAIRS + 1, 8, 128), f32),
            pltpu.VMEM((nvar, PAIRS, 8, 128), f32),
            pltpu.VMEM((PAIRS, 8, 128), f32),
            pltpu.VMEM((2, nvar * OWN, 8, 128), f32),
            pltpu.VMEM((2, 2, nvar * OWN, 8, 128), f32),
            pltpu.VMEM(((nvar + 1) * OWN, 8, 128), f32),
            pltpu.VMEM((2, (nvar + 1) * OWN, 8, 128), f32),
            pltpu.VMEM((streams, nvar, ROWS, cols), f32),
            dma((5,)),
            dma((2, streams)),
            dma((2, streams)),
            dma((2, 2)),
            dma((2, 2)),
            dma((2,)),
            dma((2,)),
            dma((streams,)),
            dma((streams,)),
            dma,
        ],
        compiler_params=pltpu.CompilerParams(collective_id=0, has_side_effects=True),
        name="march",
    )(inflow, shape, amp, coupling, omega, rec_coef, rec_order, zone.reshape(1, 1), mask)


def solution(mesh):
    placed = (
        P(None, None, None, "cross", None),
        P(None, "cross", None),
        P("stream", None, None),
        P(),
        P(),
        P(),
        P(),
        P("stream"),
        P("cross", None),
    )

    def whole(inflow, source_shape, source_amp, coupling, omega, rec_coef, rec_order, station_zone, solid_mask):
        streams = mesh.shape["stream"]
        crosses = mesh.shape["cross"]
        dims = (
            streams,
            crosses,
            inflow.shape[1],
            inflow.shape[2],
            coupling.shape[0],
            station_zone.shape[0],
        )
        return jax.shard_map(
            functools.partial(on_device, dims),
            mesh=mesh,
            in_specs=placed,
            out_specs=P("stream", None, None, None, "cross", None),
            check_vma=False,
        )(inflow, source_shape, source_amp, coupling, omega, rec_coef, rec_order, station_zone, solid_mask)

    return whole
```

```python
import functools

import jax
import jax.numpy as jnp
from jax import lax
from jax.experimental import pallas as pl
from jax.experimental.pallas import tpu as pltpu
from jax.sharding import PartitionSpec as P

viscosity = 0.05
penalty = 0.5
damping = 0.03

MESH = pl.DeviceIdType.MESH
ROWS = 8
OWN = 4
RECUR = 4
REACH = 2
STEP = REACH * ROWS // RECUR
LEVELS = STEP * RECUR
HERE = 8 * REACH
PAIRS = HERE + OWN
SIDE = 4
ORDER = (0, 1, 0, 1, 2, 3, 2, 3, 4, 4)


def kernel(
    dims,
    inflow,
    shape,
    amp,
    coupling_in,
    omega,
    rec_coef,
    rec_order,
    zone,
    mask,
    out,
    nat_in,
    shape_in,
    mask_in,
    coupling,
    tile,
    amp_all,
    zone_all,
    mix32,
    mix,
    coef,
    field,
    packed,
    frame_src,
    frame_damp,
    sent,
    got,
    sent_fix,
    got_fix,
    exits,
    in_sem,
    gather_send,
    gather_recv,
    halo_send,
    halo_recv,
    fix_send,
    fix_recv,
    exit_send,
    exit_recv,
    local_sem,
):
    streams, crosses, freqs, nvar, zones, stations = dims
    me = lax.axis_index("stream")
    row = lax.axis_index("cross")
    freq = lax.div(me, SIDE) * 2 + lax.rem(me, 2)
    part = lax.rem(lax.div(me, 2), 2)
    above = [row >= n for n in range(1, REACH + 1)]
    below = [row < crosses - n for n in range(1, REACH + 1)]

    sub = lax.broadcasted_iota(jnp.int32, (8, 128), 0)
    lane = lax.broadcasted_iota(jnp.int32, (8, 128), 1)
    top = (sub & 2) == 0
    real = (sub & 1) == 0
    first = lane == 0
    last = lane == 127

    def swap_rows(x):
        return jnp.where(top, pltpu.roll(x, 6, 0), pltpu.roll(x, 2, 0))

    def swap_parts(x):
        return jnp.where(real, pltpu.roll(x, 7, 0), pltpu.roll(x, 1, 0))

    loads = [
        pltpu.make_async_copy(inflow.at[:, freq], nat_in, in_sem.at[0]),
        pltpu.make_async_copy(shape, shape_in, in_sem.at[1]),
        pltpu.make_async_copy(mask, mask_in, in_sem.at[2]),
        pltpu.make_async_copy(amp.at[0], amp_all.at[me], in_sem.at[3]),
        pltpu.make_async_copy(zone, zone_all.at[me], in_sem.at[4]),
        pltpu.make_async_copy(coupling_in, coupling, in_sem.at[5]),
    ]
    for load in loads:
        load.start()

    barrier = pltpu.get_barrier_semaphore()

    def greet(k, carry):
        pl.semaphore_signal(
            barrier,
            inc=1,
            device_id=(lax.rem(me + k, streams), row),
            device_id_type=MESH,
        )
        return carry

    for n in range(REACH):

        @pl.when(above[n])
        def _():
            pl.semaphore_signal(barrier, inc=1, device_id=(me, row - 1 - n), device_id_type=MESH)

        @pl.when(below[n])
        def _():
            pl.semaphore_signal(barrier, inc=1, device_id=(me, row + 1 + n), device_id_type=MESH)

    lax.fori_loop(1, streams, greet, 0)

    for n in range(REACH):
        for missing, at in ((~above[n], 0), (~below[n], 1)):

            @pl.when(missing)
            def _():
                for slot in range(2):
                    got[slot, n, at] = jnp.zeros_like(got[slot, n, at])
                got_fix[n, at] = jnp.zeros_like(got_fix[n, at])

    side = jnp.where(top, 1.0, -1.0).astype(jnp.float32)
    same = (lane & 7) == sub
    spots = {}
    for kind in range(3):
        for w in range(nvar):
            for t in range(2):
                eights = [
                    10 * kind + g - 16 * t
                    for g in range(10)
                    if ORDER[g] == w and 0 <= 10 * kind + g - 16 * t < 16
                ]
                if eights:
                    hit = functools.reduce(
                        jnp.logical_or, [lax.shift_right_logical(lane, 3) == g for g in eights]
                    )
                    spots[kind, w, t] = hit & same

    loads[5].wait()

    def zone_mix(z, carry):
        def full(value):
            return jnp.full((8, 128), value, jnp.float32)

        table = {}
        for i in range(nvar):
            for w in range(i, nvar):
                rows_iw = full(0.25 * (coupling[z, 0, i, w] + coupling[z, 0, w, i])) * side
                cols_iw = 0.25 * (coupling[z, 1, i, w] + coupling[z, 1, w, i])
                dot = coupling[z, 3, i, 0] * coupling[z, 3, w, 0]
                for k in range(1, nvar):
                    dot = dot + coupling[z, 3, i, k] * coupling[z, 3, w, k]
                if i == w:
                    dot = dot + 1.0
                visc = viscosity * dot
                turn = 0.5 * (coupling[z, 2, i, w] - coupling[z, 2, w, i])
                around = (visc + rows_iw, visc - rows_iw, full(visc + cols_iw), full(visc - cols_iw))
                table[i, w] = (full(turn - 4.0 * visc),) + around
                table[w, i] = (full(-turn - 4.0 * visc),) + around
        for i in range(nvar):
            for block, kinds in ((0, (0, 1, 2)), (1, (3,)), (2, (4,))):
                for t in range(2):
                    value = jnp.zeros((8, 128), jnp.float32)
                    for place, kind in enumerate(kinds):
                        for w in range(nvar):
                            if (place, w, t) in spots:
                                value = jnp.where(spots[place, w, t], table[i, w][kind], value)
                    high = value.astype(jnp.bfloat16).astype(jnp.float32)
                    at = 8 * (2 * nvar * block + i)
                    mix32[at : at + 8, 128 * t : 128 * t + 128] = high
                    at = at + 8 * nvar
                    mix32[at : at + 8, 128 * t : 128 * t + 128] = value - high
        mix[z] = mix32[...].astype(jnp.bfloat16)
        return carry

    lax.fori_loop(0, zones, zone_mix, 0)

    f0, f1, f2, f3 = [rec_coef[rec_order[k]] * (1.0 / (4 - k)) for k in range(4)]
    spin = omega[freq]
    c1 = f3
    c2 = c1 * f2
    c3 = c2 * f1
    c4 = c3 * f0
    spin2 = spin * spin
    spin3 = spin2 * spin
    re_part = [1.0 - c2 * spin2 + c4 * spin2 * spin2, c1 - 3.0 * c3 * spin2, c2 - 6.0 * c4 * spin2, c3, c4]
    im_part = [c3 * spin3 - c1 * spin, 4.0 * c4 * spin3 - 2.0 * c2 * spin, -3.0 * c3 * spin, -4.0 * c4 * spin]
    flip = jnp.where(real, 1.0, -1.0).astype(jnp.float32)
    for k in range(5):
        coef[k] = jnp.full((8, 128), re_part[k], jnp.float32)
    for k in range(4):
        coef[5 + k] = jnp.full((8, 128), im_part[k], jnp.float32) * flip

    def halves(x, y=None):
        both = x if y is None else jnp.concatenate([x, y], axis=0)
        high = both.astype(jnp.bfloat16)
        wide = high.astype(jnp.float32)
        low = both - wide
        if y is None:
            return jnp.concatenate([wide, low], axis=0).astype(jnp.bfloat16)
        return high, low.astype(jnp.bfloat16)

    def pack(level, j, xs):
        for v in range(0, nvar - 1, 2):
            high, low = halves(xs[v], xs[v + 1])
            packed[level, j, 16 * v : 16 * v + 16] = high
            packed[level, j, 16 * v + 16 : 16 * v + 32] = low
        packed[level, j, 16 * nvar - 16 : 16 * nvar] = halves(xs[nvar - 1])

    def keep(level, j, xs):
        for v in range(nvar):
            field[level, v, j] = xs[v]
        if level < LEVELS:
            pack(level, j, xs)
            if j == PAIRS - 1:
                pack(level, PAIRS, [swap_rows(x) for x in xs])

    def pairs_of(slot, get):
        for p in range(2):
            for h in range(2):
                tile[slot, pl.ds(4 * h + p, 8, stride=8), :] = get(p, h)
        return [
            jnp.where(top, tile[slot, 8 * k : 8 * k + 8], swap_rows(tile[slot, 56 - 8 * k : 64 - 8 * k]))
            for k in range(OWN)
        ]

    for load in loads[:5]:
        load.wait()
    own = [
        pairs_of(v, lambda p, h: nat_in[p, v, :, 128 * h : 128 * h + 128]) for v in range(nvar)
    ]
    for k in range(OWN):
        keep(0, HERE + k, [own[v][k] for v in range(nvar)])
        for v in range(nvar):
            sent[0, k * nvar + v] = own[v][k]
    for v in range(nvar):
        own = pairs_of(v, lambda p, h: shape_in[v, :, 128 * h : 128 * h + 128])
        for k in range(OWN):
            frame_src[v, HERE + k] = own[k]
            sent_fix[v * OWN + k] = own[k]
    own = pairs_of(
        0,
        lambda p, h: penalty * mask_in[:, 128 * h : 128 * h + 128].astype(jnp.float32) + damping,
    )
    for k in range(OWN):
        frame_damp[HERE + k] = own[k]
        sent_fix[nvar * OWN + k] = own[k]

    near = [x.astype(jnp.int32) for x in above + below]
    pl.semaphore_wait(barrier, streams - 1 + functools.reduce(lambda x, y: x + y, near))

    def gather_copies(k):
        peer = lax.rem(me + k, streams)
        return (
            pltpu.make_async_remote_copy(
                zone, zone_all.at[me], gather_send.at[0, k], gather_recv.at[0, k],
                device_id=(peer, row), device_id_type=MESH,
            ),
            pltpu.make_async_remote_copy(
                amp.at[0], amp_all.at[me], gather_send.at[1, k], gather_recv.at[1, k],
                device_id=(peer, row), device_id_type=MESH,
            ),
        )

    def gather_start(k, carry):
        for copy in gather_copies(k):
            copy.start()
        return carry

    lax.fori_loop(1, streams, gather_start, 0)

    def both_ways(source, target, send_sems, recv_sems, n):
        up = pltpu.make_async_remote_copy(
            source, target.at[n, 1], send_sems.at[n, 0], recv_sems.at[n, 1],
            device_id=(me, row - 1 - n), device_id_type=MESH,
        )
        down = pltpu.make_async_remote_copy(
            source, target.at[n, 0], send_sems.at[n, 1], recv_sems.at[n, 0],
            device_id=(me, row + 1 + n), device_id_type=MESH,
        )
        return up, down

    def halo(slot):
        return [
            both_ways(sent.at[slot], got.at[slot], halo_send.at[slot], halo_recv.at[slot], n)
            for n in range(REACH)
        ]

    fixed = [both_ways(sent_fix, got_fix, fix_send, fix_recv, n) for n in range(REACH)]

    def start(copies):
        for n in range(REACH):

            @pl.when(above[n])
            def _():
                copies[n][0].start()

            @pl.when(below[n])
            def _():
                copies[n][1].start()

    def wait_send(copies):
        for n in range(REACH):

            @pl.when(above[n])
            def _():
                copies[n][0].wait_send()

            @pl.when(below[n])
            def _():
                copies[n][1].wait_send()

    def wait_recv(copies):
        for n in range(REACH):

            @pl.when(above[n])
            def _():
                copies[n][1].wait_recv()

            @pl.when(below[n])
            def _():
                copies[n][0].wait_recv()

    start(halo(0))
    start(fixed)

    def halo_pairs(before, after):
        outer = [jnp.where(top, before(k), after(k)) for k in range(OWN)]
        inner = [swap_rows(jnp.where(top, after(k), before(k))) for k in range(OWN)]
        return outer + inner[::-1]

    wait_send(fixed)
    wait_recv(fixed)
    for n in range(REACH):
        base = HERE - 8 * (n + 1)
        for v in range(nvar + 1):
            pairs = halo_pairs(
                lambda k: got_fix[n, 0, v * OWN + k], lambda k: got_fix[n, 1, v * OWN + k]
            )
            for j in range(8):
                if v < nvar:
                    frame_src[v, base + j] = pairs[j]
                else:
                    frame_damp[base + j] = pairs[j]

    inside = {
        HERE - 1 - 8 * n: jnp.where(top, near[n].astype(jnp.float32), near[REACH + n].astype(jnp.float32))
        for n in range(REACH)
    }

    def gather_wait(k, carry):
        for copy in gather_copies(k):
            copy.wait()
        return carry

    lax.fori_loop(1, streams, gather_wait, 0)

    def exit_copy(n, p, source):
        return pltpu.make_async_remote_copy(
            exits.at[n, p], out.at[0, p, freq], exit_send.at[n, p], exit_recv.at[source, p],
            device_id=(n, row), device_id_type=MESH,
        )

    def exit_local(n, p):
        return pltpu.make_async_copy(exits.at[n, p], out.at[0, p, freq], local_sem.at[p])

    spot = lax.rem(me, SIDE)

    def same_line(n):
        return lax.rem(n, SIDE) == spot

    def other_lines(n):
        return lax.rem(n + me, 2) == 1

    def station(n):
        here = jnp.max(zone_all[n])
        amps = amp_all[n]
        mine = lax.broadcasted_iota(jnp.int32, amps.shape, 1) == freq
        amps = jnp.sum(jnp.where(mine, amps, 0.0), axis=1, keepdims=True)
        return here, jnp.where(real, amps[0:1], amps[1:2])

    def task(level, chunk, stations_):
        here, weight = stations_[level // RECUR]
        operands = [
            jnp.concatenate([packed[level, j], packed[level, j + 1], packed[level, j - 1]], axis=0)
            for j in chunk
        ]
        operand = operands[0] if len(chunk) == 1 else jnp.concatenate(operands, axis=1)
        result = jnp.dot(
            mix[here, :, 0 : operand.shape[0]], operand, preferred_element_type=jnp.float32
        )
        base = level // RECUR * RECUR
        for a, j in enumerate(chunk):

            def part_of(block, i):
                at = 8 * (2 * nvar * block + i)
                cols = slice(128 * a, 128 * a + 128)
                return result[at : at + 8, cols] + result[at + 8 * nvar : at + 8 * nvar + 8, cols]

            values = []
            for i in range(nvar):
                east = part_of(1, i)
                west = part_of(2, i)
                east = pltpu.roll(jnp.where(first, pltpu.roll(east, 4, 0), east), 127, 1)
                west = pltpu.roll(jnp.where(last, pltpu.roll(west, 4, 0), west), 1, 1)
                value = part_of(0, i) - frame_damp[j] * field[level, i, j] + (east + west)
                if j in inside:
                    value = value * inside[j]
                if (level + 1) % RECUR == 0:
                    u = [field[base + k, i, j] for k in range(4)]
                    a_sum = coef[0] * u[0] + coef[4] * value
                    b_sum = coef[5] * u[0]
                    for k in range(1, 4):
                        a_sum = a_sum + coef[k] * u[k]
                        b_sum = b_sum + coef[5 + k] * u[k]
                    value = a_sum + swap_parts(b_sum) + weight * frame_src[i, j]
                values.append(value)
            keep(level + 1, j, values)

    def leave(n, level):
        for v in range(nvar):
            for k in range(OWN):
                x = field[level, v, HERE + k]
                tile[v, 8 * k : 8 * k + 8] = x
                tile[v, 56 - 8 * k : 64 - 8 * k] = swap_rows(x)
            for p in range(2):
                for h in range(2):
                    exits[n, p, v, :, 128 * h : 128 * h + 128] = tile[v, pl.ds(4 * h + p, 8, stride=8), :]

        @pl.when(n == me)
        def _():
            for p in range(2):
                exit_local(n, p).start()

        @pl.when(same_line(n) & (n != me))
        def _():
            for p in range(2):
                exit_copy(n, p, me).start()

        @pl.when(other_lines(n))
        def _():
            exit_copy(n, part, me).start()

    stages = stations // STEP

    def stage(t, carry):
        slot = lax.rem(t, 2)
        other = 1 - slot
        wait_recv(halo(slot))
        for n in range(REACH):
            base = HERE - 8 * (n + 1)
            pairs = [
                halo_pairs(
                    lambda k: got[slot, n, 0, k * nvar + v], lambda k: got[slot, n, 1, k * nvar + v]
                )
                for v in range(nvar)
            ]
            for j in range(8):
                keep(0, base + j, [pairs[v][j] for v in range(nvar)])
        stations_ = [station(STEP * t + i) for i in range(STEP)]
        for level in range(LEVELS):
            todo = list(range(level + 1, PAIRS))
            chunks = [todo[a : a + 2] for a in range(len(todo) % 2, len(todo), 2)]
            if len(todo) % 2:
                chunks = [todo[:1]] + chunks
            for chunk in chunks[::-1]:
                task(level, chunk, stations_)

        @pl.when(t < stages - 1)
        def _():
            @pl.when(t > 0)
            def _():
                wait_send(halo(other))

            for v in range(nvar):
                for k in range(OWN):
                    sent[other, k * nvar + v] = field[LEVELS, v, HERE + k]
            start(halo(other))
            for k in range(OWN):
                keep(0, HERE + k, [field[LEVELS, v, HERE + k] for v in range(nvar)])

        for i in range(STEP):
            leave(STEP * t + i, RECUR * (i + 1))
        return carry

    lax.fori_loop(0, stages, stage, 0)

    if stages > 1:
        wait_send(halo((stages - 2) % 2))
    wait_send(halo((stages - 1) % 2))

    def finish(n, carry):
        @pl.when(n == me)
        def _():
            for p in range(2):
                exit_local(n, p).wait()

        @pl.when(same_line(n) & (n != me))
        def _():
            for p in range(2):
                exit_copy(n, p, n).wait_send()
                exit_copy(n, p, n).wait_recv()

        @pl.when(other_lines(n))
        def _():
            exit_copy(n, part, n).wait_send()
            theirs = lax.rem(lax.div(n, 2), 2)
            exit_copy(n, theirs, n).wait_recv()

        return carry

    lax.fori_loop(0, streams, finish, 0)


def on_device(dims, inflow, shape, amp, coupling, omega, rec_coef, rec_order, zone, mask):
    streams, crosses, freqs, nvar, zones, stations = dims
    cols = inflow.shape[-1]
    anywhere = pl.BlockSpec(memory_space=pl.ANY)
    scalars = pl.BlockSpec(memory_space=pltpu.SMEM)
    f32 = jnp.float32
    dma = pltpu.SemaphoreType.DMA
    return pl.pallas_call(
        functools.partial(kernel, dims),
        out_shape=jax.ShapeDtypeStruct((1, 2, freqs, nvar, ROWS, cols), f32),
        in_specs=[anywhere, anywhere, anywhere, anywhere, scalars, scalars, scalars, anywhere, anywhere],
        out_specs=anywhere,
        scratch_shapes=[
            pltpu.VMEM((2, nvar, ROWS, cols), f32),
            pltpu.VMEM((nvar, ROWS, cols), f32),
            pltpu.VMEM((ROWS, cols), jnp.int32),
            pltpu.SMEM((zones, 4, nvar, nvar), f32),
            pltpu.VMEM((nvar, 64, 128), f32),
            pltpu.VMEM((streams, 2, freqs), f32),
            pltpu.VMEM((streams, 1, 1), jnp.int32),
            pltpu.VMEM((48 * nvar, 256), f32),
            pltpu.VMEM((zones, 48 * nvar, 256), jnp.bfloat16),
            pltpu.VMEM((9, 8, 128), f32),
            pltpu.VMEM((LEVELS + 1, nvar, PAIRS, 8, 128), f32),
            pltpu.VMEM((LEVELS, PAIRS + 1, 16 * nvar, 128), jnp.bfloat16),
            pltpu.VMEM((nvar, PAIRS, 8, 128), f32),
            pltpu.VMEM((PAIRS, 8, 128), f32),
            pltpu.VMEM((2, nvar * OWN, 8, 128), f32),
            pltpu.VMEM((2, REACH, 2, nvar * OWN, 8, 128), f32),
            pltpu.VMEM(((nvar + 1) * OWN, 8, 128), f32),
            pltpu.VMEM((REACH, 2, (nvar + 1) * OWN, 8, 128), f32),
            pltpu.VMEM((streams, 2, nvar, ROWS, cols), f32),
            dma((6,)),
            dma((2, streams)),
            dma((2, streams)),
            dma((2, REACH, 2)),
            dma((2, REACH, 2)),
            dma((REACH, 2)),
            dma((REACH, 2)),
            dma((streams, 2)),
            dma((streams, 2)),
            dma((2,)),
        ],
        compiler_params=pltpu.CompilerParams(collective_id=0, has_side_effects=True),
        name="march",
    )(inflow, shape, amp, coupling, omega, rec_coef, rec_order, zone.reshape(1, 1), mask)


def solution(mesh):
    placed = (
        P(None, None, None, "cross", None),
        P(None, "cross", None),
        P("stream", None, None),
        P(),
        P(),
        P(),
        P(),
        P("stream"),
        P("cross", None),
    )

    def whole(inflow, source_shape, source_amp, coupling, omega, rec_coef, rec_order, station_zone, solid_mask):
        streams = mesh.shape["stream"]
        crosses = mesh.shape["cross"]
        dims = (
            streams,
            crosses,
            inflow.shape[1],
            inflow.shape[2],
            coupling.shape[0],
            station_zone.shape[0],
        )
        return jax.shard_map(
            functools.partial(on_device, dims),
            mesh=mesh,
            in_specs=placed,
            out_specs=P("stream", None, None, None, "cross", None),
            check_vma=False,
        )(inflow, source_shape, source_amp, coupling, omega, rec_coef, rec_order, station_zone, solid_mask)

    return whole
```

```python
import functools

import jax
import jax.numpy as jnp
from jax import lax
from jax.experimental import pallas as pl
from jax.experimental.pallas import tpu as pltpu
from jax.sharding import PartitionSpec as P

viscosity = 0.05
penalty = 0.5
damping = 0.03

MESH = pl.DeviceIdType.MESH
ROWS = 8
OWN = 4
RECUR = 4
REACH = 2
STEP = REACH * ROWS // RECUR
LEVELS = STEP * RECUR
HERE = 8 * REACH
PAIRS = HERE + OWN
SIDE = 4
ORDER = (0, 1, 0, 1, 2, 3, 2, 3, 4, 4)


def kernel(
    dims,
    inflow,
    shape,
    amp,
    coupling_in,
    omega,
    rec_coef,
    rec_order,
    zone,
    mask,
    out,
    nat_in,
    shape_in,
    mask_in,
    coupling,
    tile,
    amp_all,
    zone_all,
    mix32,
    mix,
    coef,
    field,
    packed,
    frame_src,
    frame_damp,
    sent,
    got,
    sent_fix,
    got_fix,
    exits,
    in_sem,
    gather_send,
    gather_recv,
    halo_send,
    halo_recv,
    fix_send,
    fix_recv,
    exit_send,
    exit_recv,
    local_sem,
):
    streams, crosses, freqs, nvar, zones, stations = dims
    me = lax.axis_index("stream")
    row = lax.axis_index("cross")
    freq = lax.div(me, SIDE) * 2 + lax.rem(me, 2)
    part = lax.rem(lax.div(me, 2), 2)
    above = [row >= n for n in range(1, REACH + 1)]
    below = [row < crosses - n for n in range(1, REACH + 1)]

    sub = lax.broadcasted_iota(jnp.int32, (8, 128), 0)
    lane = lax.broadcasted_iota(jnp.int32, (8, 128), 1)
    top = (sub & 2) == 0
    real = (sub & 1) == 0
    first = lane == 0
    last = lane == 127

    def swap_rows(x):
        return jnp.where(top, pltpu.roll(x, 6, 0), pltpu.roll(x, 2, 0))

    def swap_parts(x):
        return jnp.where(real, pltpu.roll(x, 7, 0), pltpu.roll(x, 1, 0))

    loads = [
        pltpu.make_async_copy(inflow.at[:, freq], nat_in, in_sem.at[0]),
        pltpu.make_async_copy(shape, shape_in, in_sem.at[1]),
        pltpu.make_async_copy(mask, mask_in, in_sem.at[2]),
        pltpu.make_async_copy(amp.at[0], amp_all.at[me], in_sem.at[3]),
        pltpu.make_async_copy(zone, zone_all.at[me], in_sem.at[4]),
        pltpu.make_async_copy(coupling_in, coupling, in_sem.at[5]),
    ]
    for load in loads:
        load.start()

    barrier = pltpu.get_barrier_semaphore()

    def greet(k, carry):
        pl.semaphore_signal(
            barrier,
            inc=1,
            device_id=(lax.rem(me + k, streams), row),
            device_id_type=MESH,
        )
        return carry

    for n in range(REACH):

        @pl.when(above[n])
        def _():
            pl.semaphore_signal(barrier, inc=1, device_id=(me, row - 1 - n), device_id_type=MESH)

        @pl.when(below[n])
        def _():
            pl.semaphore_signal(barrier, inc=1, device_id=(me, row + 1 + n), device_id_type=MESH)

    lax.fori_loop(1, streams, greet, 0)

    for n in range(REACH):
        for missing, at in ((~above[n], 0), (~below[n], 1)):

            @pl.when(missing)
            def _():
                for slot in range(2):
                    got[slot, n, at] = jnp.zeros_like(got[slot, n, at])
                got_fix[n, at] = jnp.zeros_like(got_fix[n, at])

    side = jnp.where(top, 1.0, -1.0).astype(jnp.float32)
    same = (lane & 7) == sub
    spots = {}
    for kind in range(3):
        for w in range(nvar):
            for t in range(2):
                eights = [
                    10 * kind + g - 16 * t
                    for g in range(10)
                    if ORDER[g] == w and 0 <= 10 * kind + g - 16 * t < 16
                ]
                if eights:
                    hit = functools.reduce(
                        jnp.logical_or, [lax.shift_right_logical(lane, 3) == g for g in eights]
                    )
                    spots[kind, w, t] = hit & same

    loads[5].wait()

    def zone_mix(z, carry):
        def full(value):
            return jnp.full((8, 128), value, jnp.float32)

        table = {}
        for i in range(nvar):
            for w in range(i, nvar):
                rows_iw = full(0.25 * (coupling[z, i, 0, w] + coupling[z, w, 0, i])) * side
                cols_iw = 0.25 * (coupling[z, i, 1, w] + coupling[z, w, 1, i])
                dot = coupling[z, i, 3, 0] * coupling[z, w, 3, 0]
                for k in range(1, nvar):
                    dot = dot + coupling[z, i, 3, k] * coupling[z, w, 3, k]
                if i == w:
                    dot = dot + 1.0
                visc = viscosity * dot
                turn = 0.5 * (coupling[z, i, 2, w] - coupling[z, w, 2, i])
                around = (visc + rows_iw, visc - rows_iw, full(visc + cols_iw), full(visc - cols_iw))
                table[i, w] = (full(turn - 4.0 * visc),) + around
                table[w, i] = (full(-turn - 4.0 * visc),) + around
        for i in range(nvar):
            for block, kinds in ((0, (0, 1, 2)), (1, (3,)), (2, (4,))):
                for t in range(2):
                    value = jnp.zeros((8, 128), jnp.float32)
                    for place, kind in enumerate(kinds):
                        for w in range(nvar):
                            if (place, w, t) in spots:
                                value = jnp.where(spots[place, w, t], table[i, w][kind], value)
                    high = value.astype(jnp.bfloat16).astype(jnp.float32)
                    at = 8 * (2 * nvar * block + i)
                    mix32[at : at + 8, 128 * t : 128 * t + 128] = high
                    at = at + 8 * nvar
                    mix32[at : at + 8, 128 * t : 128 * t + 128] = value - high
        mix[z] = mix32[...].astype(jnp.bfloat16)
        return carry

    lax.fori_loop(0, zones, zone_mix, 0)

    f0, f1, f2, f3 = [rec_coef[rec_order[k]] * (1.0 / (4 - k)) for k in range(4)]
    spin = omega[freq]
    c1 = f3
    c2 = c1 * f2
    c3 = c2 * f1
    c4 = c3 * f0
    spin2 = spin * spin
    spin3 = spin2 * spin
    re_part = [1.0 - c2 * spin2 + c4 * spin2 * spin2, c1 - 3.0 * c3 * spin2, c2 - 6.0 * c4 * spin2, c3, c4]
    im_part = [c3 * spin3 - c1 * spin, 4.0 * c4 * spin3 - 2.0 * c2 * spin, -3.0 * c3 * spin, -4.0 * c4 * spin]
    flip = jnp.where(real, 1.0, -1.0).astype(jnp.float32)
    for k in range(5):
        coef[k] = jnp.full((8, 128), re_part[k], jnp.float32)
    for k in range(4):
        coef[5 + k] = jnp.full((8, 128), im_part[k], jnp.float32) * flip

    def halves(x, y=None):
        both = x if y is None else jnp.concatenate([x, y], axis=0)
        high = both.astype(jnp.bfloat16)
        wide = high.astype(jnp.float32)
        low = both - wide
        if y is None:
            return jnp.concatenate([wide, low], axis=0).astype(jnp.bfloat16)
        return high, low.astype(jnp.bfloat16)

    def pack(level, j, xs):
        for v in range(0, nvar - 1, 2):
            high, low = halves(xs[v], xs[v + 1])
            packed[level, j, 16 * v : 16 * v + 16] = high
            packed[level, j, 16 * v + 16 : 16 * v + 32] = low
        packed[level, j, 16 * nvar - 16 : 16 * nvar] = halves(xs[nvar - 1])

    def keep(level, j, xs):
        for v in range(nvar):
            field[level, v, j] = xs[v]
        if level < LEVELS:
            pack(level, j, xs)
            if j == PAIRS - 1:
                pack(level, PAIRS, [swap_rows(x) for x in xs])

    def pairs_of(slot, get):
        for p in range(2):
            for h in range(2):
                tile[slot, pl.ds(4 * h + p, 8, stride=8), :] = get(p, h)
        return [
            jnp.where(top, tile[slot, 8 * k : 8 * k + 8], swap_rows(tile[slot, 56 - 8 * k : 64 - 8 * k]))
            for k in range(OWN)
        ]

    for load in loads[:5]:
        load.wait()
    own = [
        pairs_of(v, lambda p, h: nat_in[p, v, :, 128 * h : 128 * h + 128]) for v in range(nvar)
    ]
    for k in range(OWN):
        keep(0, HERE + k, [own[v][k] for v in range(nvar)])
        for v in range(nvar):
            sent[0, k * nvar + v] = own[v][k]
    fixes = [
        pairs_of(
            0,
            lambda p, h: penalty * mask_in[:, 128 * h : 128 * h + 128].astype(jnp.float32) + damping,
        )
    ] + [
        pairs_of(v, lambda p, h: shape_in[v, :, 128 * h : 128 * h + 128]) for v in range(nvar)
    ]
    for k in range(OWN):
        frame_damp[HERE + k] = fixes[0][k]
        for v in range(nvar):
            frame_src[v, HERE + k] = fixes[1 + v][k]
        for m in range((nvar + 1) // 2):
            sent_fix[m * OWN + k] = jnp.where(real, fixes[2 * m][k], fixes[2 * m + 1][k])

    near = [x.astype(jnp.int32) for x in above + below]
    pl.semaphore_wait(barrier, streams - 1 + functools.reduce(lambda x, y: x + y, near))

    def gather_copies(k):
        peer = lax.rem(me + k, streams)
        return (
            pltpu.make_async_remote_copy(
                zone, zone_all.at[me], gather_send.at[0, k], gather_recv.at[0, k],
                device_id=(peer, row), device_id_type=MESH,
            ),
            pltpu.make_async_remote_copy(
                amp.at[0], amp_all.at[me], gather_send.at[1, k], gather_recv.at[1, k],
                device_id=(peer, row), device_id_type=MESH,
            ),
        )

    def gather_start(k, carry):
        for copy in gather_copies(k):
            copy.start()
        return carry

    lax.fori_loop(1, streams, gather_start, 0)

    def both_ways(source, target, send_sems, recv_sems, n):
        up = pltpu.make_async_remote_copy(
            source, target.at[n, 1], send_sems.at[n, 0], recv_sems.at[n, 1],
            device_id=(me, row - 1 - n), device_id_type=MESH,
        )
        down = pltpu.make_async_remote_copy(
            source, target.at[n, 0], send_sems.at[n, 1], recv_sems.at[n, 0],
            device_id=(me, row + 1 + n), device_id_type=MESH,
        )
        return up, down

    def halo(slot):
        return [
            both_ways(sent.at[slot], got.at[slot], halo_send.at[slot], halo_recv.at[slot], n)
            for n in range(REACH)
        ]

    fixed = [both_ways(sent_fix, got_fix, fix_send, fix_recv, n) for n in range(REACH)]

    def start(copies):
        for n in range(REACH):

            @pl.when(above[n])
            def _():
                copies[n][0].start()

            @pl.when(below[n])
            def _():
                copies[n][1].start()

    def wait_send(copies):
        for n in range(REACH):

            @pl.when(above[n])
            def _():
                copies[n][0].wait_send()

            @pl.when(below[n])
            def _():
                copies[n][1].wait_send()

    def wait_recv(copies, blocks=range(REACH)):
        for n in blocks:

            @pl.when(above[n])
            def _():
                copies[n][1].wait_recv()

            @pl.when(below[n])
            def _():
                copies[n][0].wait_recv()

    start(halo(0))
    start(fixed)

    def halo_pairs(before, after):
        outer = [jnp.where(top, before(k), after(k)) for k in range(OWN)]
        inner = [swap_rows(jnp.where(top, after(k), before(k))) for k in range(OWN)]
        return outer + inner[::-1]

    wait_send(fixed)
    wait_recv(fixed)
    for n in range(REACH):
        base = HERE - 8 * (n + 1)
        for m in range((nvar + 1) // 2):
            pairs = halo_pairs(
                lambda k: got_fix[n, 0, m * OWN + k], lambda k: got_fix[n, 1, m * OWN + k]
            )
            for j in range(8):
                swapped = swap_parts(pairs[j])
                one = jnp.where(real, pairs[j], swapped)
                two = jnp.where(real, swapped, pairs[j])
                if m:
                    frame_src[2 * m - 1, base + j] = one
                else:
                    frame_damp[base + j] = one
                frame_src[2 * m, base + j] = two

    inside = {
        HERE - 1 - 8 * n: jnp.where(top, near[n].astype(jnp.float32), near[REACH + n].astype(jnp.float32))
        for n in range(REACH)
    }

    def gather_wait(k, carry):
        for copy in gather_copies(k):
            copy.wait()
        return carry

    lax.fori_loop(1, streams, gather_wait, 0)

    def exit_copy(n, p, source):
        return pltpu.make_async_remote_copy(
            exits.at[n, p], out.at[0, p, freq], exit_send.at[n, p], exit_recv.at[source, p],
            device_id=(n, row), device_id_type=MESH,
        )

    def exit_local(n, p):
        return pltpu.make_async_copy(exits.at[n, p], out.at[0, p, freq], local_sem.at[p])

    spot = lax.rem(me, SIDE)

    def same_line(n):
        return lax.rem(n, SIDE) == spot

    def other_lines(n):
        return lax.rem(n + me, 2) == 1

    def station(n):
        here = jnp.max(zone_all[n])
        amps = amp_all[n]
        mine = lax.broadcasted_iota(jnp.int32, amps.shape, 1) == freq
        amps = jnp.sum(jnp.where(mine, amps, 0.0), axis=1, keepdims=True)
        return here, jnp.where(real, amps[0:1], amps[1:2])

    def task(level, chunk, stations_):
        here, weight = stations_[level // RECUR]
        operands = [
            jnp.concatenate([packed[level, j], packed[level, j + 1], packed[level, j - 1]], axis=0)
            for j in chunk
        ]
        operand = operands[0] if len(chunk) == 1 else jnp.concatenate(operands, axis=1)
        result = jnp.dot(
            mix[here, :, 0 : operand.shape[0]], operand, preferred_element_type=jnp.float32
        )
        base = level // RECUR * RECUR
        for a, j in enumerate(chunk):

            def part_of(block, i):
                at = 8 * (2 * nvar * block + i)
                cols = slice(128 * a, 128 * a + 128)
                return result[at : at + 8, cols] + result[at + 8 * nvar : at + 8 * nvar + 8, cols]

            values = []
            for i in range(nvar):
                east = part_of(1, i)
                west = part_of(2, i)
                east = pltpu.roll(jnp.where(first, pltpu.roll(east, 4, 0), east), 127, 1)
                west = pltpu.roll(jnp.where(last, pltpu.roll(west, 4, 0), west), 1, 1)
                value = part_of(0, i) - frame_damp[j] * field[level, i, j] + (east + west)
                if j in inside:
                    value = value * inside[j]
                if (level + 1) % RECUR == 0:
                    u = [field[base + k, i, j] for k in range(4)]
                    a_sum = coef[0] * u[0] + coef[4] * value
                    b_sum = coef[5] * u[0]
                    for k in range(1, 4):
                        a_sum = a_sum + coef[k] * u[k]
                        b_sum = b_sum + coef[5 + k] * u[k]
                    value = a_sum + swap_parts(b_sum) + weight * frame_src[i, j]
                values.append(value)
            keep(level + 1, j, values)

    def leave(n, level):
        for v in range(nvar):
            for k in range(OWN):
                x = field[level, v, HERE + k]
                tile[v, 8 * k : 8 * k + 8] = x
                tile[v, 56 - 8 * k : 64 - 8 * k] = swap_rows(x)
            for p in range(2):
                for h in range(2):
                    exits[n, p, v, :, 128 * h : 128 * h + 128] = tile[v, pl.ds(4 * h + p, 8, stride=8), :]

        @pl.when(n == me)
        def _():
            for p in range(2):
                exit_local(n, p).start()

        @pl.when(same_line(n) & (n != me))
        def _():
            for p in range(2):
                exit_copy(n, p, me).start()

        @pl.when(other_lines(n))
        def _():
            exit_copy(n, part, me).start()

    stages = stations // STEP

    def stage(t, carry):
        slot = lax.rem(t, 2)
        other = 1 - slot
        stations_ = [station(STEP * t + i) for i in range(STEP)]
        done = [set() for _ in range(LEVELS + 1)]
        done[0] = set(range(HERE, PAIRS))
        own = set(range(HERE, PAIRS))
        left = set()

        def advance():
            for level in range(LEVELS):
                have = done[level] | {PAIRS}
                todo = [
                    j
                    for j in range(level + 1, PAIRS)
                    if {j - 1, j, j + 1} <= have and j not in done[level + 1]
                ]
                chunks = [todo[a : a + 2] for a in range(len(todo) % 2, len(todo), 2)]
                if len(todo) % 2:
                    chunks = [todo[:1]] + chunks
                for chunk in chunks[::-1]:
                    task(level, chunk, stations_)
                done[level + 1].update(todo)
                i = level // RECUR
                if (level + 1) % RECUR == 0 and own <= done[level + 1] and i not in left and i < STEP - 1:
                    left.add(i)
                    leave(STEP * t + i, level + 1)

        wait_recv(halo(slot))
        for n in range(REACH):
            base = HERE - 8 * (n + 1)
            pairs = [
                halo_pairs(
                    lambda k: got[slot, n, 0, k * nvar + v], lambda k: got[slot, n, 1, k * nvar + v]
                )
                for v in range(nvar)
            ]
            for j in range(8):
                keep(0, base + j, [pairs[v][j] for v in range(nvar)])
            done[0].update(range(base, base + 8))
        advance()

        @pl.when(t < stages - 1)
        def _():
            @pl.when(t > 0)
            def _():
                wait_send(halo(other))

            for v in range(nvar):
                for k in range(OWN):
                    sent[other, k * nvar + v] = field[LEVELS, v, HERE + k]
            start(halo(other))
            for k in range(OWN):
                keep(0, HERE + k, [field[LEVELS, v, HERE + k] for v in range(nvar)])

        leave(STEP * t + STEP - 1, LEVELS)
        return carry

    lax.fori_loop(0, stages, stage, 0)

    if stages > 1:
        wait_send(halo((stages - 2) % 2))
    wait_send(halo((stages - 1) % 2))

    def finish(n, carry):
        @pl.when(n == me)
        def _():
            for p in range(2):
                exit_local(n, p).wait()

        @pl.when(same_line(n) & (n != me))
        def _():
            for p in range(2):
                exit_copy(n, p, n).wait_send()
                exit_copy(n, p, n).wait_recv()

        @pl.when(other_lines(n))
        def _():
            exit_copy(n, part, n).wait_send()
            theirs = lax.rem(lax.div(n, 2), 2)
            exit_copy(n, theirs, n).wait_recv()

        return carry

    lax.fori_loop(0, streams, finish, 0)


def on_device(dims, inflow, shape, amp, coupling, omega, rec_coef, rec_order, zone, mask):
    streams, crosses, freqs, nvar, zones, stations = dims
    cols = inflow.shape[-1]
    anywhere = pl.BlockSpec(memory_space=pl.ANY)
    scalars = pl.BlockSpec(memory_space=pltpu.SMEM)
    f32 = jnp.float32
    dma = pltpu.SemaphoreType.DMA
    return pl.pallas_call(
        functools.partial(kernel, dims),
        out_shape=jax.ShapeDtypeStruct((1, 2, freqs, nvar, ROWS, cols), f32),
        in_specs=[anywhere, anywhere, anywhere, anywhere, scalars, scalars, scalars, anywhere, anywhere],
        out_specs=anywhere,
        scratch_shapes=[
            pltpu.VMEM((2, nvar, ROWS, cols), f32),
            pltpu.VMEM((nvar, ROWS, cols), f32),
            pltpu.VMEM((ROWS, cols), jnp.int32),
            pltpu.SMEM((zones, nvar, 4, nvar), f32),
            pltpu.VMEM((nvar, 64, 128), f32),
            pltpu.VMEM((streams, 2, freqs), f32),
            pltpu.VMEM((streams, 1, 1), jnp.int32),
            pltpu.VMEM((48 * nvar, 256), f32),
            pltpu.VMEM((zones, 48 * nvar, 256), jnp.bfloat16),
            pltpu.VMEM((9, 8, 128), f32),
            pltpu.VMEM((LEVELS + 1, nvar, PAIRS, 8, 128), f32),
            pltpu.VMEM((LEVELS, PAIRS + 1, 16 * nvar, 128), jnp.bfloat16),
            pltpu.VMEM((nvar, PAIRS, 8, 128), f32),
            pltpu.VMEM((PAIRS, 8, 128), f32),
            pltpu.VMEM((2, nvar * OWN, 8, 128), f32),
            pltpu.VMEM((2, REACH, 2, nvar * OWN, 8, 128), f32),
            pltpu.VMEM(((nvar + 1) // 2 * OWN, 8, 128), f32),
            pltpu.VMEM((REACH, 2, (nvar + 1) // 2 * OWN, 8, 128), f32),
            pltpu.VMEM((streams, 2, nvar, ROWS, cols), f32),
            dma((6,)),
            dma((2, streams)),
            dma((2, streams)),
            dma((2, REACH, 2)),
            dma((2, REACH, 2)),
            dma((REACH, 2)),
            dma((REACH, 2)),
            dma((streams, 2)),
            dma((streams, 2)),
            dma((2,)),
        ],
        compiler_params=pltpu.CompilerParams(collective_id=0, has_side_effects=True),
        name="march",
    )(inflow, shape, amp, coupling.transpose(0, 2, 1, 3), omega, rec_coef, rec_order, zone.reshape(1, 1), mask)


def solution(mesh):
    placed = (
        P(None, None, None, "cross", None),
        P(None, "cross", None),
        P("stream", None, None),
        P(),
        P(),
        P(),
        P(),
        P("stream"),
        P("cross", None),
    )

    def whole(inflow, source_shape, source_amp, coupling, omega, rec_coef, rec_order, station_zone, solid_mask):
        streams = mesh.shape["stream"]
        crosses = mesh.shape["cross"]
        dims = (
            streams,
            crosses,
            inflow.shape[1],
            inflow.shape[2],
            coupling.shape[0],
            station_zone.shape[0],
        )
        return jax.shard_map(
            functools.partial(on_device, dims),
            mesh=mesh,
            in_specs=placed,
            out_specs=P("stream", None, None, None, "cross", None),
            check_vma=False,
        )(inflow, source_shape, source_amp, coupling, omega, rec_coef, rec_order, station_zone, solid_mask)

    return whole
```

```python
import functools

import jax
import jax.numpy as jnp
from jax import lax
from jax.experimental import pallas as pl
from jax.experimental.pallas import tpu as pltpu
from jax.sharding import PartitionSpec as P

viscosity = 0.05
penalty = 0.5
damping = 0.03

MESH = pl.DeviceIdType.MESH
ROWS = 8
OWN = 4
RECUR = 4
REACH = 2
STEP = REACH * ROWS // RECUR
LEVELS = STEP * RECUR
HERE = 8 * REACH
PAIRS = HERE + OWN
SIDE = 4
ORDER = (0, 1, 0, 1, 2, 3, 2, 3, 4, 4)


def kernel(
    dims,
    inflow,
    shape,
    amp,
    coupling_in,
    omega,
    rec_coef,
    rec_order,
    zone,
    mask,
    out,
    nat_in,
    shape_in,
    mask_in,
    coupling,
    tile,
    amp_all,
    zone_all,
    mix32,
    mix,
    coef,
    field,
    packed,
    frame_src,
    frame_damp,
    sent,
    got,
    sent_fix,
    got_fix,
    exits,
    in_sem,
    gather_send,
    gather_recv,
    halo_send,
    halo_recv,
    fix_send,
    fix_recv,
    exit_send,
    exit_recv,
    local_sem,
):
    streams, crosses, freqs, nvar, zones, stations = dims
    me = lax.axis_index("stream")
    row = lax.axis_index("cross")
    freq = lax.div(me, SIDE) * 2 + lax.rem(me, 2)
    part = lax.rem(lax.div(me, 2), 2)
    above = [row >= n for n in range(1, REACH + 1)]
    below = [row < crosses - n for n in range(1, REACH + 1)]

    sub = lax.broadcasted_iota(jnp.int32, (8, 128), 0)
    lane = lax.broadcasted_iota(jnp.int32, (8, 128), 1)
    top = (sub & 2) == 0
    real = (sub & 1) == 0
    first = lane == 0
    last = lane == 127

    def swap_rows(x):
        return jnp.where(top, pltpu.roll(x, 6, 0), pltpu.roll(x, 2, 0))

    def swap_parts(x):
        return jnp.where(real, pltpu.roll(x, 7, 0), pltpu.roll(x, 1, 0))

    loads = [
        pltpu.make_async_copy(inflow.at[:, freq], nat_in, in_sem.at[0]),
        pltpu.make_async_copy(shape, shape_in, in_sem.at[1]),
        pltpu.make_async_copy(mask, mask_in, in_sem.at[2]),
        pltpu.make_async_copy(amp.at[0], amp_all.at[me], in_sem.at[3]),
        pltpu.make_async_copy(zone, zone_all.at[me], in_sem.at[4]),
        pltpu.make_async_copy(coupling_in, coupling, in_sem.at[5]),
    ]
    barrier = pltpu.get_barrier_semaphore()

    def greet(k, carry):
        pl.semaphore_signal(
            barrier,
            inc=1,
            device_id=(lax.rem(me + k, streams), row),
            device_id_type=MESH,
        )
        return carry

    for n in range(REACH):

        @pl.when(above[n])
        def _():
            pl.semaphore_signal(barrier, inc=1, device_id=(me, row - 1 - n), device_id_type=MESH)

        @pl.when(below[n])
        def _():
            pl.semaphore_signal(barrier, inc=1, device_id=(me, row + 1 + n), device_id_type=MESH)

    lax.fori_loop(1, streams, greet, 0)

    for load in loads:
        load.start()

    for n in range(REACH):
        for missing, at in ((~above[n], 0), (~below[n], 1)):

            @pl.when(missing)
            def _():
                for slot in range(2):
                    got[slot, n, at] = jnp.zeros_like(got[slot, n, at])
                got_fix[n, at] = jnp.zeros_like(got_fix[n, at])

    def halves(x, y=None):
        both = x if y is None else jnp.concatenate([x, y], axis=0)
        high = both.astype(jnp.bfloat16)
        wide = high.astype(jnp.float32)
        low = both - wide
        if y is None:
            return jnp.concatenate([wide, low], axis=0).astype(jnp.bfloat16)
        return high, low.astype(jnp.bfloat16)

    def pack(level, j, at, xs):
        at = 16 * nvar * at
        for v in range(0, nvar - 1, 2):
            high, low = halves(xs[v], xs[v + 1])
            packed[level, j, at + 16 * v : at + 16 * v + 16] = high
            packed[level, j, at + 16 * v + 16 : at + 16 * v + 32] = low
        packed[level, j, at + 16 * nvar - 16 : at + 16 * nvar] = halves(xs[nvar - 1])

    def keep(level, j, xs):
        for v in range(nvar):
            field[level, v, j] = xs[v]
        if level < LEVELS:
            pack(level, j, 0, xs)
            if j > level:
                across = [pltpu.roll(x, 4, 0) for x in xs]
                east = [pltpu.roll(jnp.where(first, o, x), 127, 1) for o, x in zip(across, xs)]
                west = [pltpu.roll(jnp.where(last, o, x), 1, 1) for o, x in zip(across, xs)]
                pack(level, j, 1, east)
                pack(level, j, 2, west)
            if j == PAIRS - 1:
                pack(level, PAIRS, 0, [swap_rows(x) for x in xs])

    def pairs_of(slot, get):
        for p in range(2):
            for h in range(2):
                tile[slot, pl.ds(4 * h + p, 8, stride=8), :] = get(p, h)
        return [
            jnp.where(top, tile[slot, 8 * k : 8 * k + 8], swap_rows(tile[slot, 56 - 8 * k : 64 - 8 * k]))
            for k in range(OWN)
        ]

    for load in loads[:5]:
        load.wait()
    own = [
        pairs_of(v, lambda p, h: nat_in[p, v, :, 128 * h : 128 * h + 128]) for v in range(nvar)
    ]
    for k in range(OWN):
        keep(0, HERE + k, [own[v][k] for v in range(nvar)])
        for v in range(nvar):
            sent[0, k * nvar + v] = own[v][k]
    fixes = [
        pairs_of(
            0,
            lambda p, h: penalty * mask_in[:, 128 * h : 128 * h + 128].astype(jnp.float32) + damping,
        )
    ] + [
        pairs_of(v, lambda p, h: shape_in[v, :, 128 * h : 128 * h + 128]) for v in range(nvar)
    ]
    for k in range(OWN):
        frame_damp[HERE + k] = fixes[0][k]
        for v in range(nvar):
            frame_src[v, HERE + k] = fixes[1 + v][k]
        for m in range((nvar + 1) // 2):
            sent_fix[m * OWN + k] = jnp.where(real, fixes[2 * m][k], fixes[2 * m + 1][k])

    near = [x.astype(jnp.int32) for x in above + below]
    pl.semaphore_wait(barrier, streams - 1 + functools.reduce(lambda x, y: x + y, near))

    def gather_copies(k):
        peer = lax.rem(me + k, streams)
        return (
            pltpu.make_async_remote_copy(
                zone, zone_all.at[me], gather_send.at[0, k], gather_recv.at[0, k],
                device_id=(peer, row), device_id_type=MESH,
            ),
            pltpu.make_async_remote_copy(
                amp.at[0], amp_all.at[me], gather_send.at[1, k], gather_recv.at[1, k],
                device_id=(peer, row), device_id_type=MESH,
            ),
        )

    def gather_start(k, carry):
        for copy in gather_copies(k):
            copy.start()
        return carry


    def both_ways(source, target, send_sems, recv_sems, n):
        up = pltpu.make_async_remote_copy(
            source, target.at[n, 1], send_sems.at[n, 0], recv_sems.at[n, 1],
            device_id=(me, row - 1 - n), device_id_type=MESH,
        )
        down = pltpu.make_async_remote_copy(
            source, target.at[n, 0], send_sems.at[n, 1], recv_sems.at[n, 0],
            device_id=(me, row + 1 + n), device_id_type=MESH,
        )
        return up, down

    def halo(slot):
        return [
            both_ways(sent.at[slot], got.at[slot], halo_send.at[slot], halo_recv.at[slot], n)
            for n in range(REACH)
        ]

    fixed = [both_ways(sent_fix, got_fix, fix_send, fix_recv, n) for n in range(REACH)]

    def start(copies):
        for n in range(REACH):

            @pl.when(above[n])
            def _():
                copies[n][0].start()

            @pl.when(below[n])
            def _():
                copies[n][1].start()

    def wait_send(copies):
        for n in range(REACH):

            @pl.when(above[n])
            def _():
                copies[n][0].wait_send()

            @pl.when(below[n])
            def _():
                copies[n][1].wait_send()

    def wait_recv(copies, blocks=range(REACH)):
        for n in blocks:

            @pl.when(above[n])
            def _():
                copies[n][1].wait_recv()

            @pl.when(below[n])
            def _():
                copies[n][0].wait_recv()

    start(fixed)
    start(halo(0))
    lax.fori_loop(1, streams, gather_start, 0)

    side = jnp.where(top, 1.0, -1.0).astype(jnp.float32)
    same = (lane & 7) == sub
    spots = {}
    for kind in range(5):
        for w in range(nvar):
            for t in range(4):
                eights = [
                    10 * kind + g - 16 * t
                    for g in range(10)
                    if ORDER[g] == w and 0 <= 10 * kind + g - 16 * t < 16
                ]
                if eights:
                    hit = functools.reduce(
                        jnp.logical_or, [lax.shift_right_logical(lane, 3) == g for g in eights]
                    )
                    spots[kind, w, t] = hit & same

    loads[5].wait()

    def zone_mix(z, carry):
        def full(value):
            return jnp.full((8, 128), value, jnp.float32)

        table = {}
        for i in range(nvar):
            for w in range(i, nvar):
                rows_iw = full(0.25 * (coupling[z, i, 0, w] + coupling[z, w, 0, i])) * side
                cols_iw = 0.25 * (coupling[z, i, 1, w] + coupling[z, w, 1, i])
                dot = coupling[z, i, 3, 0] * coupling[z, w, 3, 0]
                for k in range(1, nvar):
                    dot = dot + coupling[z, i, 3, k] * coupling[z, w, 3, k]
                if i == w:
                    dot = dot + 1.0
                visc = viscosity * dot
                turn = 0.5 * (coupling[z, i, 2, w] - coupling[z, w, 2, i])
                around = (full(visc + cols_iw), full(visc - cols_iw), visc + rows_iw, visc - rows_iw)
                table[i, w] = (full(turn - 4.0 * visc),) + around
                table[w, i] = (full(-turn - 4.0 * visc),) + around
        for i in range(nvar):
            for t in range(4):
                value = jnp.zeros((8, 128), jnp.float32)
                for kind in range(5):
                    for w in range(nvar):
                        if (kind, w, t) in spots:
                            value = jnp.where(spots[kind, w, t], table[i, w][kind], value)
                high = value.astype(jnp.bfloat16).astype(jnp.float32)
                mix32[8 * i : 8 * i + 8, 128 * t : 128 * t + 128] = high
                mix32[8 * (nvar + i) : 8 * (nvar + i) + 8, 128 * t : 128 * t + 128] = value - high
        mix[z] = mix32[...].astype(jnp.bfloat16)
        return carry

    lax.fori_loop(0, zones, zone_mix, 0)

    f0, f1, f2, f3 = [rec_coef[rec_order[k]] * (1.0 / (4 - k)) for k in range(4)]
    spin = omega[freq]
    c1 = f3
    c2 = c1 * f2
    c3 = c2 * f1
    c4 = c3 * f0
    spin2 = spin * spin
    spin3 = spin2 * spin
    re_part = [1.0 - c2 * spin2 + c4 * spin2 * spin2, c1 - 3.0 * c3 * spin2, c2 - 6.0 * c4 * spin2, c3, c4]
    im_part = [c3 * spin3 - c1 * spin, 4.0 * c4 * spin3 - 2.0 * c2 * spin, -3.0 * c3 * spin, -4.0 * c4 * spin]
    flip = jnp.where(real, 1.0, -1.0).astype(jnp.float32)
    for k in range(5):
        coef[k] = jnp.full((8, 128), re_part[k], jnp.float32)
    for k in range(4):
        coef[5 + k] = jnp.full((8, 128), im_part[k], jnp.float32) * flip

    def halo_pairs(before, after):
        outer = [jnp.where(top, before(k), after(k)) for k in range(OWN)]
        inner = [swap_rows(jnp.where(top, after(k), before(k))) for k in range(OWN)]
        return outer + inner[::-1]

    wait_send(fixed)
    wait_recv(fixed)
    for n in range(REACH):
        base = HERE - 8 * (n + 1)
        for m in range((nvar + 1) // 2):
            pairs = halo_pairs(
                lambda k: got_fix[n, 0, m * OWN + k], lambda k: got_fix[n, 1, m * OWN + k]
            )
            for j in range(8):
                swapped = swap_parts(pairs[j])
                one = jnp.where(real, pairs[j], swapped)
                two = jnp.where(real, swapped, pairs[j])
                if m:
                    frame_src[2 * m - 1, base + j] = one
                else:
                    frame_damp[base + j] = one
                frame_src[2 * m, base + j] = two

    inside = {
        HERE - 1 - 8 * n: jnp.where(top, near[n].astype(jnp.float32), near[REACH + n].astype(jnp.float32))
        for n in range(REACH)
    }

    def gather_wait(k, carry):
        for copy in gather_copies(k):
            copy.wait()
        return carry

    lax.fori_loop(1, streams, gather_wait, 0)

    def exit_copy(n, p, source):
        return pltpu.make_async_remote_copy(
            exits.at[n, p], out.at[0, p, freq], exit_send.at[n, p], exit_recv.at[source, p],
            device_id=(n, row), device_id_type=MESH,
        )

    def exit_local(n, p):
        return pltpu.make_async_copy(exits.at[n, p], out.at[0, p, freq], local_sem.at[p])

    spot = lax.rem(me, SIDE)

    def same_line(n):
        return lax.rem(n, SIDE) == spot

    def other_lines(n):
        return lax.rem(n + me, 2) == 1

    def station(n):
        here = jnp.max(zone_all[n])
        amps = amp_all[n]
        mine = lax.broadcasted_iota(jnp.int32, amps.shape, 1) == freq
        amps = jnp.sum(jnp.where(mine, amps, 0.0), axis=1, keepdims=True)
        return here, jnp.where(real, amps[0:1], amps[1:2])

    def task(level, chunk, stations_):
        here, weight = stations_[level // RECUR]
        operands = [
            jnp.concatenate(
                [
                    packed[level, j],
                    packed[level, j + 1, 0 : 16 * nvar],
                    packed[level, j - 1, 0 : 16 * nvar],
                ],
                axis=0,
            )
            for j in chunk
        ]
        operand = operands[0] if len(chunk) == 1 else jnp.concatenate(operands, axis=1)
        result = jnp.dot(
            mix[here, :, 0 : operand.shape[0]], operand, preferred_element_type=jnp.float32
        )
        base = level // RECUR * RECUR
        for a, j in enumerate(chunk):

            cols = slice(128 * a, 128 * a + 128)
            values = []
            for i in range(nvar):
                value = result[8 * i : 8 * i + 8, cols] + result[8 * (nvar + i) : 8 * (nvar + i) + 8, cols]
                value = value - frame_damp[j] * field[level, i, j]
                if j in inside:
                    value = value * inside[j]
                if (level + 1) % RECUR == 0:
                    u = [field[base + k, i, j] for k in range(4)]
                    a_sum = coef[0] * u[0] + coef[4] * value
                    b_sum = coef[5] * u[0]
                    for k in range(1, 4):
                        a_sum = a_sum + coef[k] * u[k]
                        b_sum = b_sum + coef[5 + k] * u[k]
                    value = a_sum + swap_parts(b_sum) + weight * frame_src[i, j]
                values.append(value)
            keep(level + 1, j, values)

    def leave(n, level):
        for v in range(nvar):
            for k in range(OWN):
                x = field[level, v, HERE + k]
                tile[v, 8 * k : 8 * k + 8] = x
                tile[v, 56 - 8 * k : 64 - 8 * k] = swap_rows(x)
            for p in range(2):
                for h in range(2):
                    exits[n, p, v, :, 128 * h : 128 * h + 128] = tile[v, pl.ds(4 * h + p, 8, stride=8), :]

        @pl.when(n == me)
        def _():
            for p in range(2):
                exit_local(n, p).start()

        @pl.when(same_line(n) & (n != me))
        def _():
            for p in range(2):
                exit_copy(n, p, me).start()

        @pl.when(other_lines(n))
        def _():
            exit_copy(n, part, me).start()

    stages = stations // STEP

    def stage(t, carry):
        slot = lax.rem(t, 2)
        other = 1 - slot
        stations_ = [station(STEP * t + i) for i in range(STEP)]
        done = [set() for _ in range(LEVELS + 1)]
        done[0] = set(range(HERE, PAIRS))
        own = set(range(HERE, PAIRS))
        left = set()

        def advance():
            for level in range(LEVELS):
                have = done[level] | {PAIRS}
                todo = [
                    j
                    for j in range(level + 1, PAIRS)
                    if {j - 1, j, j + 1} <= have and j not in done[level + 1]
                ]
                chunks = [todo[a : a + 2] for a in range(len(todo) % 2, len(todo), 2)]
                if len(todo) % 2:
                    chunks = [todo[:1]] + chunks
                for chunk in chunks[::-1]:
                    task(level, chunk, stations_)
                done[level + 1].update(todo)
                i = level // RECUR
                if (level + 1) % RECUR == 0 and own <= done[level + 1] and i not in left and i < STEP - 1:
                    left.add(i)
                    leave(STEP * t + i, level + 1)

        wait_recv(halo(slot))
        for n in range(REACH):
            base = HERE - 8 * (n + 1)
            pairs = [
                halo_pairs(
                    lambda k: got[slot, n, 0, k * nvar + v], lambda k: got[slot, n, 1, k * nvar + v]
                )
                for v in range(nvar)
            ]
            for j in range(8):
                keep(0, base + j, [pairs[v][j] for v in range(nvar)])
            done[0].update(range(base, base + 8))
        advance()

        @pl.when(t < stages - 1)
        def _():
            @pl.when(t > 0)
            def _():
                wait_send(halo(other))

            for v in range(nvar):
                for k in range(OWN):
                    sent[other, k * nvar + v] = field[LEVELS, v, HERE + k]
            start(halo(other))
            for k in range(OWN):
                keep(0, HERE + k, [field[LEVELS, v, HERE + k] for v in range(nvar)])

        leave(STEP * t + STEP - 1, LEVELS)
        return carry

    lax.fori_loop(0, stages, stage, 0)

    if stages > 1:
        wait_send(halo((stages - 2) % 2))
    wait_send(halo((stages - 1) % 2))

    def finish(n, carry):
        @pl.when(n == me)
        def _():
            for p in range(2):
                exit_local(n, p).wait()

        @pl.when(same_line(n) & (n != me))
        def _():
            for p in range(2):
                exit_copy(n, p, n).wait_send()
                exit_copy(n, p, n).wait_recv()

        @pl.when(other_lines(n))
        def _():
            exit_copy(n, part, n).wait_send()
            theirs = lax.rem(lax.div(n, 2), 2)
            exit_copy(n, theirs, n).wait_recv()

        return carry

    lax.fori_loop(0, streams, finish, 0)


def on_device(dims, inflow, shape, amp, coupling, omega, rec_coef, rec_order, zone, mask):
    streams, crosses, freqs, nvar, zones, stations = dims
    cols = inflow.shape[-1]
    anywhere = pl.BlockSpec(memory_space=pl.ANY)
    scalars = pl.BlockSpec(memory_space=pltpu.SMEM)
    f32 = jnp.float32
    dma = pltpu.SemaphoreType.DMA
    return pl.pallas_call(
        functools.partial(kernel, dims),
        out_shape=jax.ShapeDtypeStruct((1, 2, freqs, nvar, ROWS, cols), f32),
        in_specs=[anywhere, anywhere, anywhere, anywhere, scalars, scalars, scalars, anywhere, anywhere],
        out_specs=anywhere,
        scratch_shapes=[
            pltpu.VMEM((2, nvar, ROWS, cols), f32),
            pltpu.VMEM((nvar, ROWS, cols), f32),
            pltpu.VMEM((ROWS, cols), jnp.int32),
            pltpu.SMEM((zones, nvar, 4, nvar), f32),
            pltpu.VMEM((nvar, 64, 128), f32),
            pltpu.VMEM((streams, 2, freqs), f32),
            pltpu.VMEM((streams, 1, 1), jnp.int32),
            pltpu.VMEM((16 * nvar, 512), f32),
            pltpu.VMEM((zones, 16 * nvar, 512), jnp.bfloat16),
            pltpu.VMEM((9, 8, 128), f32),
            pltpu.VMEM((LEVELS + 1, nvar, PAIRS, 8, 128), f32),
            pltpu.VMEM((LEVELS, PAIRS + 1, 48 * nvar, 128), jnp.bfloat16),
            pltpu.VMEM((nvar, PAIRS, 8, 128), f32),
            pltpu.VMEM((PAIRS, 8, 128), f32),
            pltpu.VMEM((2, nvar * OWN, 8, 128), f32),
            pltpu.VMEM((2, REACH, 2, nvar * OWN, 8, 128), f32),
            pltpu.VMEM(((nvar + 1) // 2 * OWN, 8, 128), f32),
            pltpu.VMEM((REACH, 2, (nvar + 1) // 2 * OWN, 8, 128), f32),
            pltpu.VMEM((streams, 2, nvar, ROWS, cols), f32),
            dma((6,)),
            dma((2, streams)),
            dma((2, streams)),
            dma((2, REACH, 2)),
            dma((2, REACH, 2)),
            dma((REACH, 2)),
            dma((REACH, 2)),
            dma((streams, 2)),
            dma((streams, 2)),
            dma((2,)),
        ],
        compiler_params=pltpu.CompilerParams(collective_id=0, has_side_effects=True),
        name="march",
    )(inflow, shape, amp, coupling.transpose(0, 2, 1, 3), omega, rec_coef, rec_order, zone.reshape(1, 1), mask)


def solution(mesh):
    placed = (
        P(None, None, None, "cross", None),
        P(None, "cross", None),
        P("stream", None, None),
        P(),
        P(),
        P(),
        P(),
        P("stream"),
        P("cross", None),
    )

    def whole(inflow, source_shape, source_amp, coupling, omega, rec_coef, rec_order, station_zone, solid_mask):
        streams = mesh.shape["stream"]
        crosses = mesh.shape["cross"]
        dims = (
            streams,
            crosses,
            inflow.shape[1],
            inflow.shape[2],
            coupling.shape[0],
            station_zone.shape[0],
        )
        return jax.shard_map(
            functools.partial(on_device, dims),
            mesh=mesh,
            in_specs=placed,
            out_specs=P("stream", None, None, None, "cross", None),
            check_vma=False,
        )(inflow, source_shape, source_amp, coupling, omega, rec_coef, rec_order, station_zone, solid_mask)

    return whole
```
